32 devices in a mesh: node: 4 (over y, x), leaf: 8 (over z, core).
Axes of the slice: x: 2, y: 2, z: 4, core: 2. Of those that a mesh axis runs over, the one named last changes fastest.
Arguments:
- density: bfloat16 [128, 8, 128, 256], P('leaf', 'node'), parts along dimension 1, may hold values from -6 to 6
- near_tiles: bfloat16 [128, 6, 8, 128, 128], P('leaf', None, 'node'), parts along dimension 2, may hold values from -0.15625 to 0.15625
- neighbours: int32 [128, 6], P('leaf'), may hold values from 0 to 127, as said below
- counts: int32 [128], P('leaf'), may hold values from 3 to 6, as said below
- leaf_basis: bfloat16 [128, 8, 32, 128], P('leaf', 'node'), parts along dimension 1, may hold values from -0.375 to 0.375
- leaf_transfer: float32 [128, 8, 32, 32], P('leaf', 'node'), parts along dimension 1, may hold values from -0.1875 to 0.1875
- admissible: int32 [8, 7], P('leaf'), may hold values from 0 to 7, as said below
- top_out: float32 [8, 8, 32, 32], P('leaf', 'node'), parts along dimension 1, may hold values from -0.75 to 0.75
- top_in: float32 [8, 8, 32, 32], P('leaf', 'node'), parts along dimension 1, may hold values from -0.25 to 0.25
- coupling: float32 [8, 7, 8, 32, 32], P('leaf', None, 'node'), parts along dimension 2, may hold values from -0.25 to 0.25
- down_transfer: float32 [128, 8, 32, 32], P('leaf', 'node'), parts along dimension 1, may hold values from -0.75 to 0.75
- out_basis: bfloat16 [128, 8, 32, 128], P('leaf', 'node'), parts along dimension 1, may hold values from -0.75 to 0.75
Outputs:
- potential: bfloat16 [128, 8, 128, 256], P('leaf', 'node'), parts along dimension 1
The draws below stay inside these ranges and needn't reach their ends.
There are 4 independent parts, one for each index of `node`. The reference program is written for one: setup_inputs(seed, part) draws one part's arguments, and reference() takes and returns one part's arrays. A program takes and returns all parts, laid end to end along the dimension named above; an argument that names none is the same for every part. Nothing has to cross between parts.
Inputs may be any that keep to these rules, and one draw needn't show every extreme that they name: `neighbours`: slot 0 is the leaf itself; every neighbour lies within 4 leaf indices of its leaf; slots 1 and 2 are the leaves 4 below and above, clipped to the surface's range. `counts`: the number of live leading slots of each leaf. `admissible`: the 7 entries of row d are distinct and differ from d; slot 0 is d - 1 and slot 1 is d + 1, both modulo 8.
All inputs are finite; a program needn't handle non-finite values.
Results may differ from the reference program's by a relative error of at most 0.0045.
Values may be sent and summed in bfloat16 or wider, within the bound.
A program may use at most 128 MiB of HBM per device.

```python
import jax
import jax.numpy as jnp
from jax import lax

LEAVES_DEV = 16
B = 128
K = 32
RHS = 256
NEAR = 6
HALO = 4
SUBTREES = 8
LEAVES = 128
FAR = 7


def draw_neighbours(key, part):
    inner = jnp.concatenate([jnp.arange(-HALO + 1, 0, dtype=jnp.int32), jnp.arange(1, HALO, dtype=jnp.int32)])
    fixed_offsets = jnp.array([0, -HALO, HALO], dtype=jnp.int32)

    def one_leaf(leaf_key):
        order = jax.random.permutation(leaf_key, 2 * HALO - 2)[:NEAR - 3]
        return jnp.concatenate([fixed_offsets, inner[order]])
    offsets = jax.vmap(one_leaf)(jax.random.split(key, LEAVES))
    leaf_ids = jnp.arange(LEAVES, dtype=jnp.int32)[:, None]
    return jnp.clip(leaf_ids + offsets, 0, LEAVES - 1).astype(jnp.int32)


def draw_counts(key, part):
    load_key, extra_key, busy_key = jax.random.split(jax.random.fold_in(key, 7), 3)
    loads = jax.random.randint(load_key, (SUBTREES,), 0, NEAR - 2)
    extra = jax.random.randint(extra_key, (SUBTREES, LEAVES_DEV), 0, 1 << 20) % (loads[:, None] + 1)
    result = 3 + extra
    busiest = jax.random.randint(busy_key, (), 0, SUBTREES)
    subtree_ids = jnp.arange(SUBTREES)[:, None]
    leaf_ids = jnp.arange(LEAVES_DEV)[None, :]
    result = jnp.where((subtree_ids == busiest) & (leaf_ids == 0), NEAR, result)
    return result.reshape(LEAVES).astype(jnp.int32)


def draw_admissible(key, part):

    def one_subtree(sub_key, subtree):
        order = jax.random.permutation(sub_key, SUBTREES - 3)[:FAR - 2]
        rest = (subtree + 2 + order) % SUBTREES
        sides = jnp.stack([(subtree + SUBTREES - 1) % SUBTREES, (subtree + 1) % SUBTREES])
        return jnp.concatenate([sides, rest])
    keys = jax.random.split(jax.random.fold_in(key, 11), SUBTREES)
    return jax.vmap(one_subtree)(keys, jnp.arange(SUBTREES, dtype=jnp.int32)).astype(jnp.int32)


def levels(own_key, dims, cuts, low, high):
    gain, own = 1.0, jax.random.fold_in(own_key, 6)
    for dim, blocks in cuts:
        steps = jnp.exp(jax.random.uniform(jax.random.fold_in(own, dim), (blocks,), jnp.float32, low / len(cuts), high / len(cuts)))
        gain = gain * jnp.repeat(steps, dims[dim] // blocks).reshape([-1 if axis == dim else 1 for axis in range(len(dims))])
    return gain


def scatter_about(stream_key, shape, width, bound, cuts=(), held_as=jnp.bfloat16):
    drawn = jax.random.normal(stream_key, shape, jnp.float32) * width
    if len(cuts) > 0:
        drawn = levels(stream_key, shape, cuts, -0.22, 0.18) * drawn
    return jnp.clip(drawn, min=-bound, max=bound).astype(held_as)


def setup_inputs(seed: int = 0, part: int = 0) -> dict:
    streams_of = jax.random.split(jax.random.key(seed), 13)
    own_keys = jax.random.split(jax.random.fold_in(streams_of[12], part), 13)
    density = scatter_about(own_keys[0], (LEAVES, 2, B, RHS), 1.0, 6.0, ((0, 8),))
    near_tiles = scatter_about(own_keys[1], (LEAVES, NEAR, 2, B, B), (2 * B * NEAR) ** -0.5, 0.15625, ((0, 8),))
    neighbours = draw_neighbours(jax.random.fold_in(streams_of[12], 71), part)
    counts = draw_counts(jax.random.fold_in(streams_of[12], 71), part)
    leaf_basis = scatter_about(own_keys[4], (LEAVES, 2, K, B), (2 * B) ** -0.5, 0.375, ((0, 8),))
    leaf_transfer = scatter_about(own_keys[5], (LEAVES, 2, K, K), (2 * K * LEAVES_DEV) ** -0.5, 0.1875, ((0, 8),), jnp.float32)
    admissible = draw_admissible(jax.random.fold_in(streams_of[12], 71), part)
    top_out = scatter_about(own_keys[7], (SUBTREES, 2, K, K), (2 * K) ** -0.5, 0.75, ((0, 8),), jnp.float32)
    top_in = scatter_about(own_keys[8], (SUBTREES, 2, K, K), (2 * K * SUBTREES) ** -0.5, 0.25, ((0, 8),), jnp.float32)
    coupling = scatter_about(own_keys[9], (SUBTREES, FAR, 2, K, K), (2 * K * FAR) ** -0.5, 0.25, ((0, 8),), jnp.float32)
    down_transfer = scatter_about(own_keys[10], (LEAVES, 2, K, K), (2 * K) ** -0.5, 0.75, ((0, 8),), jnp.float32)
    out_basis = scatter_about(own_keys[11], (LEAVES, 2, K, B), (2 * K) ** -0.5, 0.75, ((0, 8),))
    return {"density": density, "near_tiles": near_tiles, "neighbours": neighbours, "counts": counts, "leaf_basis": leaf_basis, "leaf_transfer": leaf_transfer, "admissible": admissible, "top_out": top_out, "top_in": top_in, "coupling": coupling, "down_transfer": down_transfer, "out_basis": out_basis}


def complex_product(pattern, first, second, precision):
    def single(left_side, right_side):
        return jnp.einsum(pattern, left_side, right_side, precision=precision, preferred_element_type=jnp.float32)
    return (single(first[0], second[0]) - single(first[1], second[1]),
            single(first[0], second[1]) + single(first[1], second[0]))


def reference(density, near_tiles, neighbours, counts, leaf_basis, leaf_transfer, admissible, top_out, top_in, coupling, down_transfer, out_basis):
    highest = lax.Precision.HIGHEST
    dens_full = density.astype(jnp.float32)
    basis_full = leaf_basis.astype(jnp.float32)
    coef = complex_product('lkb,lbr->lkr', (basis_full[:, 0], basis_full[:, 1]), (dens_full[:, 0], dens_full[:, 1]), highest)
    coef = tuple(part.reshape(SUBTREES, LEAVES_DEV, K, RHS) for part in coef)
    upward = leaf_transfer.reshape(SUBTREES, LEAVES_DEV, 2, K, K)
    root = complex_product('dlij,dljr->dir', (upward[:, :, 0], upward[:, :, 1]), coef, highest)
    top_terms = complex_product('dij,djr->dir', (top_out[:, 0], top_out[:, 1]), root, highest)
    top = (jnp.sum(top_terms[0], axis=0), jnp.sum(top_terms[1], axis=0))
    picked = (root[0][admissible], root[1][admissible])
    far_field = complex_product('dfij,dfjr->dir', (coupling[:, :, 0], coupling[:, :, 1]), picked, highest)
    top_part = complex_product('dij,jr->dir', (top_in[:, 0], top_in[:, 1]), top, highest)
    far_field = (far_field[0] + top_part[0], far_field[1] + top_part[1])
    downward = down_transfer.reshape(SUBTREES, LEAVES_DEV, 2, K, K)
    down_pair = complex_product('dlij,djr->dlir', (downward[:, :, 0], downward[:, :, 1]), far_field, highest)
    down_coefs = jnp.stack([down_pair[0], down_pair[1]], axis=2).reshape(LEAVES, 2, K, RHS).astype(jnp.bfloat16)
    down_coefs = lax.optimization_barrier(down_coefs).astype(jnp.float32)
    out_full = out_basis.astype(jnp.float32)
    far_part = complex_product('lkb,lkr->lbr', (out_full[:, 0], out_full[:, 1]), (down_coefs[:, 0], down_coefs[:, 1]), highest)
    near_real = jnp.zeros((LEAVES, B, RHS), jnp.float32)
    near_imag = jnp.zeros((LEAVES, B, RHS), jnp.float32)
    for column in range(NEAR):
        pieces = density[neighbours[:, column]].astype(jnp.float32)
        tiles = near_tiles[:, column].astype(jnp.float32)
        term = complex_product('lab,lbr->lar', (tiles[:, 0], tiles[:, 1]), (pieces[:, 0], pieces[:, 1]), highest)
        live_mask = (counts > column).astype(jnp.float32)[:, None, None]
        near_real = near_real + live_mask * term[0]
        near_imag = near_imag + live_mask * term[1]
    return jnp.stack([far_part[0] + near_real, far_part[1] + near_imag], axis=1).astype(jnp.bfloat16)
```

```python
import functools

import jax
import jax.numpy as jnp
from jax import lax
from jax.experimental import pallas as pl
from jax.experimental.pallas import tpu as pltpu
from jax.sharding import PartitionSpec as P

HALO = 4
MESH = pl.DeviceIdType.MESH
F32 = jnp.float32
BF16 = jnp.bfloat16


def mul(left, right):
    return jnp.dot(left, right, preferred_element_type=F32)


def split(x):
    high = x.astype(BF16)
    return high, (x - high.astype(F32)).astype(BF16)


def pack(real, imag):
    rh, rl = split(real)
    ih, il = split(imag)
    return jnp.concatenate([rh, ih, rl, il], axis=1)


def operand(real, imag):
    minus = -imag
    left = jnp.concatenate([real, minus, real, minus], axis=0)
    right = jnp.concatenate([imag, real, imag, real], axis=0)
    return jnp.concatenate([left, right], axis=1)


def kernel(
    n,
    density,
    near_tiles,
    neighbours,
    counts,
    leaf_basis,
    leaf_transfer,
    admissible,
    top_out,
    top_in,
    coupling,
    down_transfer,
    out_basis,
    out,
    own,
    low,
    high,
    tiles,
    coef,
    msg,
    near,
    down,
    result,
    own_sem,
    tile_sem,
    side_sem,
    halo_send,
    halo_recv,
    root_send,
    root_recv,
    pass_send,
    pass_recv,
    out_sem,
):
    me = lax.axis_index("leaf")
    chips = n // 2
    chip = me // 2
    core = me % 2
    sibling = chip * 2 + (1 - core)
    leaves, _, panels, rhs = density.shape
    slots = near_tiles.shape[1]
    rank = leaf_basis.shape[2]
    far = coupling.shape[1]
    size = 2 * panels
    chunks = leaves // HALO
    inner = list(range(1, chunks - 1))
    order = inner + [0, chunks - 1]

    own_copies = [
        pltpu.make_async_copy(
            density.at[pl.ds(k * HALO, HALO)], own.at[pl.ds(k * HALO, HALO)], own_sem.at[k]
        )
        for k in range(chunks)
    ]
    tile_copies = [
        pltpu.make_async_copy(
            near_tiles.at[pl.ds(k * HALO, HALO)], tiles.at[pl.ds(k * HALO, HALO)], tile_sem.at[k]
        )
        for k in range(chunks)
    ]
    side_copies = [
        pltpu.make_async_copy(
            density.at[pl.ds(0, 2 * HALO)], low.at[pl.ds(HALO, 2 * HALO)], side_sem.at[0]
        ),
        pltpu.make_async_copy(
            density.at[pl.ds(leaves - 2 * HALO, 2 * HALO)],
            high.at[pl.ds(0, 2 * HALO)],
            side_sem.at[1],
        ),
    ]
    for copy in own_copies:
        copy.start()

    barrier = pltpu.get_barrier_semaphore()
    for step in range(1, n):
        pl.semaphore_signal(
            barrier, inc=1, device_id={"leaf": lax.rem(me + step, n)}, device_id_type=MESH
        )
    pl.semaphore_wait(barrier, n - 1)

    def halo_copy(source, target, which, to):
        return pltpu.make_async_remote_copy(
            src_ref=source,
            dst_ref=target,
            send_sem=halo_send.at[which],
            recv_sem=halo_recv.at[which],
            device_id={"leaf": to},
            device_id_type=MESH,
        )

    def to_below():
        return halo_copy(
            density.at[pl.ds(0, HALO)],
            high.at[pl.ds(2 * HALO, HALO)],
            1,
            lax.rem(me + n - 1, n),
        )

    def to_above():
        return halo_copy(
            density.at[pl.ds(leaves - HALO, HALO)], low.at[pl.ds(0, HALO)], 0, lax.rem(me + 1, n)
        )

    @pl.when(me > 0)
    def _():
        to_below().start()

    @pl.when(me < n - 1)
    def _():
        to_above().start()

    for k in order:
        tile_copies[k].start()
    for copy in side_copies:
        copy.start()

    def one_coef(leaf, carry):
        basis = leaf_basis[leaf]
        left = jnp.concatenate(
            [
                jnp.concatenate([basis[0], -basis[1]], axis=1),
                jnp.concatenate([basis[1], basis[0]], axis=1),
            ],
            axis=0,
        )
        value = mul(left, own[leaf].reshape(size, rhs))
        rows = pl.ds(pl.multiple_of(leaf * rank, rank), rank)
        coef[0, rows] = value[:rank]
        coef[1, rows] = value[rank:]
        return carry

    for k in range(chunks):
        own_copies[k].wait()
        lax.fori_loop(k * HALO, (k + 1) * HALO, one_coef, 0, unroll=True)

    upward = jnp.concatenate(
        [leaf_transfer[leaf].reshape(2 * rank, rank) for leaf in range(leaves)], axis=1
    )
    up_high, up_low = split(upward)
    up_both = jnp.concatenate([up_high, up_low], axis=0)

    def upward_sum(part):
        c_high, c_low = split(coef[part])
        first = mul(up_both, c_high)
        return first[: 2 * rank] + first[2 * rank :] + mul(up_high, c_low)

    sum_real, sum_imag = upward_sum(0), upward_sum(1)
    msg[me, :rank] = (sum_real[:rank] - sum_imag[rank:]).astype(BF16)
    msg[me, rank : 2 * rank] = (sum_real[rank:] + sum_imag[:rank]).astype(BF16)
    packed = pack(top_out[0, 0], top_out[0, 1])
    msg[me, 2 * rank :] = jnp.concatenate([packed[: rank // 2], packed[rank // 2 :]], axis=1)

    def root_copy(slot, send, recv, to):
        return pltpu.make_async_remote_copy(
            src_ref=msg.at[slot],
            dst_ref=msg.at[slot],
            send_sem=send,
            recv_sem=recv,
            device_id={"leaf": to},
            device_id_type=MESH,
        )

    direct = [root_copy(me, pass_send.at[0], pass_recv.at[0], sibling)]
    for step in range(1, chips):
        to = lax.rem(chip + step, chips) * 2 + core
        direct.append(root_copy(me, root_send.at[step], root_recv.at[step], to))
    for copy in direct:
        copy.start()

    def near_leaf(source, shift):
        first = me * leaves + shift
        count = source.shape[0]

        def body(leaf, carry):
            tops, bottoms, pieces = [], [], []
            for slot in range(slots):
                live = jnp.where(counts[leaf] > slot, 1.0, 0.0).astype(F32)
                live = jnp.full((panels, panels), live, F32).astype(BF16)
                real = tiles[leaf, slot, 0] * live
                imag = tiles[leaf, slot, 1] * live
                tops += [real, -imag]
                bottoms += [imag, real]
                place = jnp.clip(neighbours[slot, leaf] - first, 0, count - 1)
                pieces.append(source[place].reshape(size, rhs))
            left = jnp.concatenate(
                [jnp.concatenate(tops, axis=1), jnp.concatenate(bottoms, axis=1)], axis=0
            )
            near[leaf] = mul(left, jnp.concatenate(pieces, axis=0))
            return carry

        return body

    for k in inner:
        tile_copies[k].wait()
        lax.fori_loop(k * HALO, (k + 1) * HALO, near_leaf(own, 0), 0)

    passed = []
    for step in range(1, chips):
        slot = lax.rem(chip + chips - step, chips) * 2 + core
        direct[step].wait_recv()
        copy = root_copy(slot, pass_send.at[step], pass_recv.at[step], sibling)
        copy.start()
        passed.append(copy)

    tile_copies[0].wait()
    side_copies[0].wait()

    @pl.when(me > 0)
    def _():
        to_above().wait_recv()

    lax.fori_loop(0, HALO, near_leaf(low, -HALO), 0)
    tile_copies[chunks - 1].wait()
    side_copies[1].wait()

    @pl.when(me < n - 1)
    def _():
        to_below().wait_recv()

    lax.fori_loop(leaves - HALO, leaves, near_leaf(high, leaves - 2 * HALO), 0)

    d_high, d_low = split(down_transfer[...].reshape(leaves * 2 * rank, rank))
    downward = jnp.concatenate([d_high, d_low, d_high], axis=1)
    pairs = [pack(coupling[0, slot, 0], coupling[0, slot, 1]) for slot in range(far)]
    packed_in = pack(top_in[0, 0], top_in[0, 1])

    direct[0].wait_recv()
    for copy in passed:
        copy.wait_recv()

    tops, roots = [], []
    for d in range(n):
        piece = msg[d, 2 * rank :]
        tops.append(jnp.concatenate([piece[:, : size // 2], piece[:, size // 2 :]], axis=0))
        roots.append(operand(msg[d, :rank], msg[d, rank : 2 * rank]))
    top = mul(jnp.concatenate(tops, axis=1), jnp.concatenate(roots, axis=0))
    top_high, top_low = split(top)
    picked = []
    for slot in range(far):
        value = msg[admissible[0, slot]]
        picked.append(operand(value[:rank], value[rank : 2 * rank]))
    field = mul(jnp.concatenate(pairs, axis=1), jnp.concatenate(picked, axis=0))
    field += mul(packed_in, operand(top_high[:, :rhs], top_high[:, rhs:]))
    field += mul(packed_in, operand(top_low[:, :rhs], top_low[:, rhs:]))
    f_high, f_low = split(field)
    down[...] = mul(downward, jnp.concatenate([f_high, f_high, f_low], axis=0))

    def finish(leaf, carry):
        rows = pl.multiple_of(leaf * 2 * rank, 2 * rank)
        upper = down[pl.ds(rows, rank)]
        lower = down[pl.ds(rows + rank, rank)]
        coefs = jnp.concatenate(
            [upper[:, :rhs] - lower[:, rhs:], lower[:, :rhs] + upper[:, rhs:]], axis=0
        ).astype(BF16)
        basis = out_basis[leaf]
        left = jnp.concatenate(
            [
                jnp.concatenate([basis[0], basis[1]], axis=1),
                jnp.concatenate([-basis[1], basis[0]], axis=1),
            ],
            axis=0,
        )
        value = lax.dot_general(left, coefs, (((0,), (0,)), ((), ())), preferred_element_type=F32)
        result[leaf] = (value + near[leaf]).astype(BF16).reshape(2, panels, rhs)
        return carry

    outs = []
    for k in range(chunks):
        lax.fori_loop(k * HALO, (k + 1) * HALO, finish, 0, unroll=True)
        copy = pltpu.make_async_copy(
            result.at[pl.ds(k * HALO, HALO)], out.at[pl.ds(k * HALO, HALO)], out_sem.at[k]
        )
        copy.start()
        outs.append(copy)

    @pl.when(me > 0)
    def _():
        to_below().wait_send()

    @pl.when(me < n - 1)
    def _():
        to_above().wait_send()

    for copy in direct + passed:
        copy.wait_send()
    for copy in outs:
        copy.wait()


def shards(*args):
    density, near_tiles = args[0], args[1]
    leaf_basis = args[4]
    n = lax.axis_size("leaf")
    leaves, _, panels, rhs = density.shape
    rank = leaf_basis.shape[2]
    chunks = leaves // HALO
    hbm = pl.BlockSpec(memory_space=pl.ANY)
    vmem = pl.BlockSpec(memory_space=pltpu.VMEM)
    smem = pl.BlockSpec(memory_space=pltpu.SMEM)
    dma = pltpu.SemaphoreType.DMA
    return pl.pallas_call(
        functools.partial(kernel, n),
        out_shape=jax.ShapeDtypeStruct(density.shape, BF16),
        in_specs=[hbm, hbm, smem, smem, vmem, vmem, smem, vmem, vmem, vmem, vmem, vmem],
        out_specs=hbm,
        scratch_shapes=[
            pltpu.VMEM(density.shape, BF16),
            pltpu.VMEM((3 * HALO,) + density.shape[1:], BF16),
            pltpu.VMEM((3 * HALO,) + density.shape[1:], BF16),
            pltpu.VMEM(near_tiles.shape, BF16),
            pltpu.VMEM((2, leaves * rank, rhs), F32),
            pltpu.VMEM((n, 2 * rank + rank // 2, rhs), BF16),
            pltpu.VMEM((leaves, 2 * panels, rhs), F32),
            pltpu.VMEM((leaves * 2 * rank, 2 * rhs), F32),
            pltpu.VMEM(density.shape, BF16),
            dma((chunks,)),
            dma((chunks,)),
            dma((2,)),
            dma((2,)),
            dma((2,)),
            dma((n // 2,)),
            dma((n // 2,)),
            dma((n // 2,)),
            dma((n // 2,)),
            dma((chunks,)),
        ],
        compiler_params=pltpu.CompilerParams(
            collective_id=0, has_side_effects=True, vmem_limit_bytes=62 * 1024 * 1024
        ),
    )(*args[:2], args[2].T, *args[3:])


def solution(mesh):
    in_specs = (
        P("leaf", "node", None, None),
        P("leaf", None, "node", None, None),
        P("leaf", None),
        P("leaf"),
        P("leaf", "node", None, None),
        P("leaf", "node", None, None),
        P("leaf", None),
        P("leaf", "node", None, None),
        P("leaf", "node", None, None),
        P("leaf", None, "node", None, None),
        P("leaf", "node", None, None),
        P("leaf", "node", None, None),
    )
    out_specs = P("leaf", "node", None, None)
    return jax.shard_map(shards, mesh=mesh, in_specs=in_specs, out_specs=out_specs, check_vma=False)
```

```python
import functools

import jax
import jax.numpy as jnp
from jax import lax
from jax.experimental import pallas as pl
from jax.experimental.pallas import tpu as pltpu
from jax.sharding import PartitionSpec as P

HALO = 4
LIVE = 3
INDICES = (2, 3, 6)
MESH = pl.DeviceIdType.MESH
F32 = jnp.float32
BF16 = jnp.bfloat16


def mul(left, right):
    return jnp.dot(left, right, preferred_element_type=F32)


def split(x):
    high = x.astype(BF16)
    return high, (x - high.astype(F32)).astype(BF16)


def pack(real, imag):
    rh, rl = split(real)
    ih, il = split(imag)
    return jnp.concatenate([rh, ih, rl, il], axis=1)


def operand(real, imag):
    minus = -imag
    left = jnp.concatenate([real, minus, real, minus], axis=0)
    right = jnp.concatenate([imag, real, imag, real], axis=0)
    return jnp.concatenate([left, right], axis=1)


def kernel(
    n,
    density,
    near_tiles,
    neighbours_far,
    counts_far,
    leaf_basis_far,
    leaf_transfer_far,
    admissible_far,
    top_out_far,
    top_in_far,
    coupling_far,
    down_transfer_far,
    out_basis_far,
    out,
    neighbours,
    counts,
    leaf_basis,
    leaf_transfer,
    admissible,
    top_out,
    top_in,
    coupling,
    down_transfer,
    out_basis,
    turned,
    small_sem,
    own,
    low,
    high,
    tiles,
    coef,
    msg,
    near,
    down,
    own_sem,
    tile_sem,
    side_sem,
    halo_send,
    halo_recv,
    root_send,
    root_recv,
    pass_send,
    pass_recv,
):
    me = lax.axis_index("leaf")
    chips = n // 2
    chip = me // 2
    core = me % 2
    sibling = chip * 2 + (1 - core)
    leaves, _, panels, rhs = density.shape
    slots = near_tiles.shape[1]
    rank = leaf_basis.shape[2]
    far = coupling.shape[1]
    size = 2 * panels
    chunks = leaves // HALO
    inner = list(range(1, chunks - 1))
    order = inner + [0, chunks - 1]

    own_copies = [
        pltpu.make_async_copy(
            density.at[pl.ds(k * HALO, HALO)], own.at[pl.ds(k * HALO, HALO)], own_sem.at[k]
        )
        for k in range(chunks)
    ]
    tile_copies = [
        pltpu.make_async_copy(
            near_tiles.at[pl.ds(k * HALO, HALO)], tiles.at[pl.ds(k * HALO, HALO)], tile_sem.at[k]
        )
        for k in range(chunks)
    ]
    side_copies = [
        pltpu.make_async_copy(
            density.at[pl.ds(0, 2 * HALO)], low.at[pl.ds(HALO, 2 * HALO)], side_sem.at[0]
        ),
        pltpu.make_async_copy(
            density.at[pl.ds(leaves - 2 * HALO, 2 * HALO)],
            high.at[pl.ds(0, 2 * HALO)],
            side_sem.at[1],
        ),
    ]
    small = [
        (leaf_basis_far, leaf_basis),
        (leaf_transfer_far, leaf_transfer),
        (top_out_far, top_out),
        (top_in_far, top_in),
        (coupling_far, coupling),
        (down_transfer_far, down_transfer),
        (out_basis_far, out_basis),
        (neighbours_far, neighbours),
        (counts_far, counts),
        (admissible_far, admissible),
    ]
    small_copies = [
        pltpu.make_async_copy(source, target, small_sem.at[k])
        for k, (source, target) in enumerate(small)
    ]
    barrier = pltpu.get_barrier_semaphore()
    for step in range(1, n):
        pl.semaphore_signal(
            barrier, inc=1, device_id={"leaf": lax.rem(me + step, n)}, device_id_type=MESH
        )
    small_copies[0].start()
    for copy in own_copies:
        copy.start()
    for copy in small_copies[1:]:
        copy.start()
    for k in order:
        tile_copies[k].start()
    for copy in side_copies:
        copy.start()

    def one_coef(leaf, carry):
        basis = leaf_basis[leaf]
        left = jnp.concatenate(
            [
                jnp.concatenate([basis[0], -basis[1]], axis=1),
                jnp.concatenate([basis[1], basis[0]], axis=1),
            ],
            axis=0,
        )
        value = mul(left, own[leaf].reshape(size, rhs))
        rows = pl.ds(pl.multiple_of(leaf * rank, rank), rank)
        coef[0, rows] = value[:rank]
        coef[1, rows] = value[rank:]
        return carry

    def coefs_of(k):
        own_copies[k].wait()
        lax.fori_loop(k * HALO, (k + 1) * HALO, one_coef, 0, unroll=True)

    early = chunks // 2
    small_copies[0].wait()
    for k in range(early):
        coefs_of(k)
    pl.semaphore_wait(barrier, n - 1)

    def halo_copy(source, target, which, to):
        return pltpu.make_async_remote_copy(
            src_ref=source,
            dst_ref=target,
            send_sem=halo_send.at[which],
            recv_sem=halo_recv.at[which],
            device_id={"leaf": to},
            device_id_type=MESH,
        )

    def to_below():
        return halo_copy(
            density.at[pl.ds(0, HALO)],
            high.at[pl.ds(2 * HALO, HALO)],
            1,
            lax.rem(me + n - 1, n),
        )

    def to_above():
        return halo_copy(
            density.at[pl.ds(leaves - HALO, HALO)], low.at[pl.ds(0, HALO)], 0, lax.rem(me + 1, n)
        )

    @pl.when(me > 0)
    def _():
        to_below().start()

    @pl.when(me < n - 1)
    def _():
        to_above().start()

    for k in range(early, chunks):
        coefs_of(k)
    small_copies[1].wait()
    small_copies[2].wait()
    upward = jnp.concatenate(
        [leaf_transfer[leaf].reshape(2 * rank, rank) for leaf in range(leaves)], axis=1
    )
    up_high, up_low = split(upward)
    up_both = jnp.concatenate([up_high, up_low], axis=0)

    def upward_sum(part):
        c_high, c_low = split(coef[part])
        first = mul(up_both, c_high)
        return first[: 2 * rank] + first[2 * rank :] + mul(up_high, c_low)

    sum_real, sum_imag = upward_sum(0), upward_sum(1)
    msg[me, :rank] = (sum_real[:rank] - sum_imag[rank:]).astype(BF16)
    msg[me, rank : 2 * rank] = (sum_real[rank:] + sum_imag[:rank]).astype(BF16)
    packed = pack(top_out[0, 0], top_out[0, 1])
    msg[me, 2 * rank :] = jnp.concatenate([packed[: rank // 2], packed[rank // 2 :]], axis=1)

    def root_copy(slot, send, recv, to):
        return pltpu.make_async_remote_copy(
            src_ref=msg.at[slot],
            dst_ref=msg.at[slot],
            send_sem=send,
            recv_sem=recv,
            device_id={"leaf": to},
            device_id_type=MESH,
        )

    direct = [root_copy(me, pass_send.at[0], pass_recv.at[0], sibling)]
    for step in range(1, chips):
        to = lax.rem(chip + step, chips) * 2 + core
        direct.append(root_copy(me, root_send.at[step], root_recv.at[step], to))
    for copy in direct:
        copy.start()

    def near_leaf(source, shift):
        first = me * leaves + shift
        count = source.shape[0]

        def body(leaf, carry):
            tops, bottoms, pieces = [], [], []
            for slot in range(slots):
                real = tiles[leaf, slot, 0]
                imag = tiles[leaf, slot, 1]
                if slot >= LIVE:
                    live = jnp.where(counts[leaf] > slot, 1.0, 0.0).astype(F32)
                    live = jnp.full((panels, panels), live, F32).astype(BF16)
                    real *= live
                    imag *= live
                tops += [real, -imag]
                bottoms += [imag, real]
                place = jnp.clip(neighbours[slot, leaf] - first, 0, count - 1)
                pieces.append(source[place].reshape(size, rhs))
            left = jnp.concatenate(
                [jnp.concatenate(tops, axis=1), jnp.concatenate(bottoms, axis=1)], axis=0
            )
            near[leaf] = mul(left, jnp.concatenate(pieces, axis=0))
            return carry

        return body

    small_copies[7].wait()
    small_copies[8].wait()
    for k in inner:
        tile_copies[k].wait()
        lax.fori_loop(k * HALO, (k + 1) * HALO, near_leaf(own, 0), 0, unroll=2)

    small_copies[6].wait()

    def turn(leaf, carry):
        basis = out_basis[leaf].astype(F32)
        left = jnp.concatenate([basis[0], -basis[1]], axis=0)
        right = jnp.concatenate([basis[1], basis[0]], axis=0)
        turned[leaf] = jnp.concatenate([left, right], axis=1).T.astype(BF16)
        return carry

    lax.fori_loop(0, leaves, turn, 0, unroll=2)

    passed = []
    for step in range(1, chips):
        slot = lax.rem(chip + chips - step, chips) * 2 + core
        direct[step].wait_recv()
        copy = root_copy(slot, pass_send.at[step], pass_recv.at[step], sibling)
        copy.start()
        passed.append(copy)

    tile_copies[0].wait()
    side_copies[0].wait()

    @pl.when(me > 0)
    def _():
        to_above().wait_recv()

    lax.fori_loop(0, HALO, near_leaf(low, -HALO), 0, unroll=2)
    tile_copies[chunks - 1].wait()
    side_copies[1].wait()

    @pl.when(me < n - 1)
    def _():
        to_below().wait_recv()

    lax.fori_loop(leaves - HALO, leaves, near_leaf(high, leaves - 2 * HALO), 0, unroll=2)

    for copy in small_copies[3:6] + small_copies[9:]:
        copy.wait()
    d_high, d_low = split(down_transfer[...].reshape(leaves * 2 * rank, rank))
    downward = jnp.concatenate([d_high, d_low, d_high], axis=1)
    pairs = [pack(coupling[0, slot, 0], coupling[0, slot, 1]) for slot in range(far)]
    packed_in = pack(top_in[0, 0], top_in[0, 1])

    direct[0].wait_recv()
    for copy in passed:
        copy.wait_recv()

    tops, roots = [], []
    for d in range(n):
        piece = msg[d, 2 * rank :]
        tops.append(jnp.concatenate([piece[:, : size // 2], piece[:, size // 2 :]], axis=0))
        roots.append(operand(msg[d, :rank], msg[d, rank : 2 * rank]))
    top = mul(jnp.concatenate(tops, axis=1), jnp.concatenate(roots, axis=0))
    top_high, top_low = split(top)
    picked = []
    for slot in range(far):
        value = msg[admissible[0, slot]]
        picked.append(operand(value[:rank], value[rank : 2 * rank]))
    field = mul(jnp.concatenate(pairs, axis=1), jnp.concatenate(picked, axis=0))
    field += mul(packed_in, operand(top_high[:, :rhs], top_high[:, rhs:]))
    field += mul(packed_in, operand(top_low[:, :rhs], top_low[:, rhs:]))
    f_high, f_low = split(field)
    down[...] = mul(downward, jnp.concatenate([f_high, f_high, f_low], axis=0))

    def finish(leaf, carry):
        rows = pl.multiple_of(leaf * 2 * rank, 2 * rank)
        upper = down[pl.ds(rows, rank)]
        lower = down[pl.ds(rows + rank, rank)]
        coefs = jnp.concatenate(
            [upper[:, :rhs] - lower[:, rhs:], lower[:, :rhs] + upper[:, rhs:]], axis=0
        ).astype(BF16)
        value = mul(turned[leaf], coefs)
        out[leaf] = (value + near[leaf]).astype(BF16).reshape(2, panels, rhs)
        return carry

    lax.fori_loop(0, leaves, finish, 0, unroll=4)

    @pl.when(me > 0)
    def _():
        to_below().wait_send()

    @pl.when(me < n - 1)
    def _():
        to_above().wait_send()

    for copy in direct + passed:
        copy.wait_send()


def shards(*args):
    density, near_tiles = args[0], args[1]
    leaf_basis = args[4]
    n = lax.axis_size("leaf")
    leaves, _, panels, rhs = density.shape
    rank = leaf_basis.shape[2]
    chunks = leaves // HALO
    hbm = pl.BlockSpec(memory_space=pltpu.HBM)
    vmem = pl.BlockSpec(memory_space=pltpu.VMEM)
    dma = pltpu.SemaphoreType.DMA
    operands = [args[2].T if k == 2 else arg for k, arg in enumerate(args)]
    for k in range(len(operands)):
        operands[k] = pltpu.with_memory_space_constraint(operands[k], pltpu.HBM)
    return pl.pallas_call(
        functools.partial(kernel, n),
        out_shape=jax.ShapeDtypeStruct(density.shape, BF16),
        in_specs=[hbm] * len(operands),
        out_specs=vmem,
        scratch_shapes=[
            (pltpu.SMEM if k in INDICES else pltpu.VMEM)(operands[k].shape, operands[k].dtype)
            for k in range(2, len(operands))
        ]
        + [
            pltpu.VMEM((leaves, 2 * panels, 2 * rank), BF16),
            dma((len(operands) - 2,)),
            pltpu.VMEM(density.shape, BF16),
            pltpu.VMEM((3 * HALO,) + density.shape[1:], BF16),
            pltpu.VMEM((3 * HALO,) + density.shape[1:], BF16),
            pltpu.VMEM(near_tiles.shape, BF16),
            pltpu.VMEM((2, leaves * rank, rhs), F32),
            pltpu.VMEM((n, 2 * rank + rank // 2, rhs), BF16),
            pltpu.VMEM((leaves, 2 * panels, rhs), F32),
            pltpu.VMEM((leaves * 2 * rank, 2 * rhs), F32),
            dma((chunks,)),
            dma((chunks,)),
            dma((2,)),
            dma((2,)),
            dma((2,)),
            dma((n // 2,)),
            dma((n // 2,)),
            dma((n // 2,)),
            dma((n // 2,)),
        ],
        compiler_params=pltpu.CompilerParams(
            collective_id=0, has_side_effects=True, vmem_limit_bytes=40 * 1024 * 1024
        ),
    )(*operands)


def solution(mesh):
    in_specs = (
        P("leaf", "node", None, None),
        P("leaf", None, "node", None, None),
        P("leaf", None),
        P("leaf"),
        P("leaf", "node", None, None),
        P("leaf", "node", None, None),
        P("leaf", None),
        P("leaf", "node", None, None),
        P("leaf", "node", None, None),
        P("leaf", None, "node", None, None),
        P("leaf", "node", None, None),
        P("leaf", "node", None, None),
    )
    out_specs = P("leaf", "node", None, None)
    return jax.shard_map(shards, mesh=mesh, in_specs=in_specs, out_specs=out_specs, check_vma=False)
```

```python
import functools

import jax
import jax.numpy as jnp
from jax import lax
from jax.experimental import pallas as pl
from jax.experimental.pallas import tpu as pltpu
from jax.sharding import PartitionSpec as P

HALO = 4
LIVE = 3
INDICES = (2, 3, 6)
MESH = pl.DeviceIdType.MESH
F32 = jnp.float32
BF16 = jnp.bfloat16


def mul(left, right):
    return jnp.dot(left, right, preferred_element_type=F32)


def split(x):
    high = x.astype(BF16)
    return high, (x - high.astype(F32)).astype(BF16)


def pack(real, imag):
    rh, rl = split(real)
    ih, il = split(imag)
    return jnp.concatenate([rh, ih, rl, il], axis=1)


def operand(real, imag):
    minus = -imag
    left = jnp.concatenate([real, minus, real, minus], axis=0)
    right = jnp.concatenate([imag, real, imag, real], axis=0)
    return jnp.concatenate([left, right], axis=1)


def kernel(
    n,
    density,
    near_tiles,
    neighbours_far,
    counts_far,
    leaf_basis_far,
    leaf_transfer_far,
    admissible_far,
    top_out_far,
    top_in_far,
    coupling_far,
    down_transfer_far,
    out_basis_far,
    out,
    neighbours,
    counts,
    leaf_basis,
    leaf_transfer,
    admissible,
    top_out,
    top_in,
    coupling,
    down_transfer,
    out_basis,
    turned,
    downward,
    paired,
    packed_in,
    small_sem,
    own,
    low,
    high,
    tiles,
    coef,
    msg,
    near,
    down,
    own_sem,
    tile_sem,
    side_sem,
    halo_send,
    halo_recv,
    root_send,
    root_recv,
    pass_send,
    pass_recv,
):
    me = lax.axis_index("leaf")
    chips = n // 2
    chip = me // 2
    core = me % 2
    sibling = chip * 2 + (1 - core)
    leaves, _, panels, rhs = density.shape
    slots = near_tiles.shape[1]
    rank = leaf_basis.shape[2]
    far = coupling.shape[1]
    size = 2 * panels
    chunks = leaves // HALO
    inner = list(range(1, chunks - 1))
    order = inner + [0, chunks - 1]

    own_copies = [
        pltpu.make_async_copy(
            density.at[pl.ds(k * HALO, HALO)], own.at[pl.ds(k * HALO, HALO)], own_sem.at[k]
        )
        for k in range(chunks)
    ]
    tile_copies = [
        pltpu.make_async_copy(
            near_tiles.at[pl.ds(k * HALO, HALO)], tiles.at[pl.ds(k * HALO, HALO)], tile_sem.at[k]
        )
        for k in range(chunks)
    ]
    side_copies = [
        pltpu.make_async_copy(
            density.at[pl.ds(0, 2 * HALO)], low.at[pl.ds(HALO, 2 * HALO)], side_sem.at[0]
        ),
        pltpu.make_async_copy(
            density.at[pl.ds(leaves - 2 * HALO, 2 * HALO)],
            high.at[pl.ds(0, 2 * HALO)],
            side_sem.at[1],
        ),
    ]
    small = [
        (leaf_basis_far, leaf_basis),
        (leaf_transfer_far, leaf_transfer),
        (top_out_far, top_out),
        (top_in_far, top_in),
        (coupling_far, coupling),
        (down_transfer_far, down_transfer),
        (out_basis_far, out_basis),
        (neighbours_far, neighbours),
        (counts_far, counts),
        (admissible_far, admissible),
    ]
    small_copies = [
        pltpu.make_async_copy(source, target, small_sem.at[k])
        for k, (source, target) in enumerate(small)
    ]
    barrier = pltpu.get_barrier_semaphore()
    for step in range(1, n):
        pl.semaphore_signal(
            barrier, inc=1, device_id={"leaf": lax.rem(me + step, n)}, device_id_type=MESH
        )
    small_copies[0].start()
    for copy in own_copies:
        copy.start()
    for copy in small_copies[1:]:
        copy.start()
    for k in order:
        tile_copies[k].start()
    for copy in side_copies:
        copy.start()

    def one_coef(leaf, carry):
        basis = leaf_basis[leaf]
        left = jnp.concatenate(
            [
                jnp.concatenate([basis[0], -basis[1]], axis=1),
                jnp.concatenate([basis[1], basis[0]], axis=1),
            ],
            axis=0,
        )
        value = mul(left, own[leaf].reshape(size, rhs))
        rows = pl.ds(pl.multiple_of(leaf * rank, rank), rank)
        coef[0, rows] = value[:rank]
        coef[1, rows] = value[rank:]
        return carry

    def coefs_of(k):
        own_copies[k].wait()
        lax.fori_loop(k * HALO, (k + 1) * HALO, one_coef, 0, unroll=True)

    pl.semaphore_wait(barrier, n - 1)

    def halo_copy(source, target, which, to):
        return pltpu.make_async_remote_copy(
            src_ref=source,
            dst_ref=target,
            send_sem=halo_send.at[which],
            recv_sem=halo_recv.at[which],
            device_id={"leaf": to},
            device_id_type=MESH,
        )

    def to_below():
        return halo_copy(
            density.at[pl.ds(0, HALO)],
            high.at[pl.ds(2 * HALO, HALO)],
            1,
            lax.rem(me + n - 1, n),
        )

    def to_above():
        return halo_copy(
            density.at[pl.ds(leaves - HALO, HALO)], low.at[pl.ds(0, HALO)], 0, lax.rem(me + 1, n)
        )

    @pl.when(me > 0)
    def _():
        to_below().start()

    @pl.when(me < n - 1)
    def _():
        to_above().start()

    small_copies[0].wait()
    for k in range(chunks):
        coefs_of(k)
    small_copies[1].wait()
    small_copies[2].wait()
    upward = jnp.concatenate(
        [leaf_transfer[leaf].reshape(2 * rank, rank) for leaf in range(leaves)], axis=1
    )
    up_high, up_low = split(upward)
    up_both = jnp.concatenate([up_high, up_low], axis=0)

    def upward_sum(part):
        c_high, c_low = split(coef[part])
        first = mul(up_both, c_high)
        return first[: 2 * rank] + first[2 * rank :] + mul(up_high, c_low)

    sum_real, sum_imag = upward_sum(0), upward_sum(1)
    msg[me, :rank] = (sum_real[:rank] - sum_imag[rank:]).astype(BF16)
    msg[me, rank : 2 * rank] = (sum_real[rank:] + sum_imag[:rank]).astype(BF16)
    packed = pack(top_out[0, 0], top_out[0, 1])
    msg[me, 2 * rank :] = jnp.concatenate([packed[: rank // 2], packed[rank // 2 :]], axis=1)

    def root_copy(slot, send, recv, to):
        return pltpu.make_async_remote_copy(
            src_ref=msg.at[slot],
            dst_ref=msg.at[slot],
            send_sem=send,
            recv_sem=recv,
            device_id={"leaf": to},
            device_id_type=MESH,
        )

    direct = [root_copy(me, pass_send.at[0], pass_recv.at[0], sibling)]
    for step in range(1, chips):
        to = lax.rem(chip + step, chips) * 2 + core
        direct.append(root_copy(me, root_send.at[step], root_recv.at[step], to))
    for copy in direct:
        copy.start()

    def near_leaf(source, shift):
        first = me * leaves + shift
        count = source.shape[0]

        def body(leaf, carry):
            tops, bottoms, pieces = [], [], []
            for slot in range(slots):
                real = tiles[leaf, slot, 0]
                imag = tiles[leaf, slot, 1]
                if slot >= LIVE:
                    live = jnp.where(counts[leaf] > slot, 1.0, 0.0).astype(F32)
                    live = jnp.full((panels, panels), live, F32).astype(BF16)
                    real *= live
                    imag *= live
                tops += [real, -imag]
                bottoms += [imag, real]
                place = jnp.clip(neighbours[slot, leaf] - first, 0, count - 1)
                pieces.append(source[place].reshape(size, rhs))
            left = jnp.concatenate(
                [jnp.concatenate(tops, axis=1), jnp.concatenate(bottoms, axis=1)], axis=0
            )
            near[leaf] = mul(left, jnp.concatenate(pieces, axis=0))
            return carry

        return body

    small_copies[7].wait()
    small_copies[8].wait()
    for k in inner:
        tile_copies[k].wait()
        lax.fori_loop(k * HALO, (k + 1) * HALO, near_leaf(own, 0), 0, unroll=2)

    small_copies[6].wait()

    def turn(leaf, carry):
        basis = out_basis[leaf].astype(F32)
        left = jnp.concatenate([basis[0], -basis[1]], axis=0)
        right = jnp.concatenate([basis[1], basis[0]], axis=0)
        turned[leaf] = jnp.concatenate([left, right], axis=1).T.astype(BF16)
        return carry

    lax.fori_loop(0, leaves, turn, 0, unroll=2)

    for copy in small_copies[3:6] + small_copies[9:]:
        copy.wait()
    d_high, d_low = split(down_transfer[...].reshape(leaves * 2 * rank, rank))
    downward[...] = jnp.concatenate([d_high, d_low, d_high], axis=1)
    pairs = [pack(coupling[0, slot, 0], coupling[0, slot, 1]) for slot in range(far)]
    packed_in[...] = pack(top_in[0, 0], top_in[0, 1])
    paired[...] = jnp.concatenate(pairs, axis=1)

    tile_copies[0].wait()
    side_copies[0].wait()

    @pl.when(me > 0)
    def _():
        to_above().wait_recv()

    lax.fori_loop(0, HALO, near_leaf(low, -HALO), 0, unroll=2)
    passed = []
    for step in range(1, chips):
        slot = lax.rem(chip + chips - step, chips) * 2 + core
        direct[step].wait_recv()
        copy = root_copy(slot, pass_send.at[step], pass_recv.at[step], sibling)
        copy.start()
        passed.append(copy)

    tile_copies[chunks - 1].wait()
    side_copies[1].wait()

    @pl.when(me < n - 1)
    def _():
        to_below().wait_recv()

    lax.fori_loop(leaves - HALO, leaves, near_leaf(high, leaves - 2 * HALO), 0, unroll=2)

    direct[0].wait_recv()
    for copy in passed:
        copy.wait_recv()

    tops, roots = [], []
    for d in range(n):
        piece = msg[d, 2 * rank :]
        tops.append(jnp.concatenate([piece[:, : size // 2], piece[:, size // 2 :]], axis=0))
        roots.append(operand(msg[d, :rank], msg[d, rank : 2 * rank]))
    top = mul(jnp.concatenate(tops, axis=1), jnp.concatenate(roots, axis=0))
    top_high, top_low = split(top)
    picked = []
    for slot in range(far):
        value = msg[admissible[0, slot]]
        picked.append(operand(value[:rank], value[rank : 2 * rank]))
    field = mul(paired[...], jnp.concatenate(picked, axis=0))
    field += mul(packed_in[...], operand(top_high[:, :rhs], top_high[:, rhs:]))
    field += mul(packed_in[...], operand(top_low[:, :rhs], top_low[:, rhs:]))
    f_high, f_low = split(field)
    down[...] = mul(downward[...], jnp.concatenate([f_high, f_high, f_low], axis=0))

    def finish(leaf, carry):
        rows = pl.multiple_of(leaf * 2 * rank, 2 * rank)
        upper = down[pl.ds(rows, rank)]
        lower = down[pl.ds(rows + rank, rank)]
        coefs = jnp.concatenate(
            [upper[:, :rhs] - lower[:, rhs:], lower[:, :rhs] + upper[:, rhs:]], axis=0
        ).astype(BF16)
        value = mul(turned[leaf], coefs)
        out[leaf] = (value + near[leaf]).astype(BF16).reshape(2, panels, rhs)
        return carry

    lax.fori_loop(0, leaves, finish, 0, unroll=4)

    @pl.when(me > 0)
    def _():
        to_below().wait_send()

    @pl.when(me < n - 1)
    def _():
        to_above().wait_send()

    for copy in direct + passed:
        copy.wait_send()


def shards(*args):
    density, near_tiles = args[0], args[1]
    leaf_basis = args[4]
    n = lax.axis_size("leaf")
    leaves, _, panels, rhs = density.shape
    rank = leaf_basis.shape[2]
    chunks = leaves // HALO
    hbm = pl.BlockSpec(memory_space=pltpu.HBM)
    vmem = pl.BlockSpec(memory_space=pltpu.VMEM)
    dma = pltpu.SemaphoreType.DMA
    operands = [args[2].T if k == 2 else arg for k, arg in enumerate(args)]
    for k in range(len(operands)):
        operands[k] = pltpu.with_memory_space_constraint(operands[k], pltpu.HBM)
    return pl.pallas_call(
        functools.partial(kernel, n),
        out_shape=jax.ShapeDtypeStruct(density.shape, BF16),
        in_specs=[hbm] * len(operands),
        out_specs=vmem,
        scratch_shapes=[
            (pltpu.SMEM if k in INDICES else pltpu.VMEM)(operands[k].shape, operands[k].dtype)
            for k in range(2, len(operands))
        ]
        + [
            pltpu.VMEM((leaves, 2 * panels, 2 * rank), BF16),
            pltpu.VMEM((leaves * 2 * rank, 3 * rank), BF16),
            pltpu.VMEM((rank, args[9].shape[1] * 4 * rank), BF16),
            pltpu.VMEM((rank, 4 * rank), BF16),
            dma((len(operands) - 2,)),
            pltpu.VMEM(density.shape, BF16),
            pltpu.VMEM((3 * HALO,) + density.shape[1:], BF16),
            pltpu.VMEM((3 * HALO,) + density.shape[1:], BF16),
            pltpu.VMEM(near_tiles.shape, BF16),
            pltpu.VMEM((2, leaves * rank, rhs), F32),
            pltpu.VMEM((n, 2 * rank + rank // 2, rhs), BF16),
            pltpu.VMEM((leaves, 2 * panels, rhs), F32),
            pltpu.VMEM((leaves * 2 * rank, 2 * rhs), F32),
            dma((chunks,)),
            dma((chunks,)),
            dma((2,)),
            dma((2,)),
            dma((2,)),
            dma((n // 2,)),
            dma((n // 2,)),
            dma((n // 2,)),
            dma((n // 2,)),
        ],
        compiler_params=pltpu.CompilerParams(
            collective_id=0, has_side_effects=True, vmem_limit_bytes=40 * 1024 * 1024
        ),
    )(*operands)


def solution(mesh):
    in_specs = (
        P("leaf", "node", None, None),
        P("leaf", None, "node", None, None),
        P("leaf", None),
        P("leaf"),
        P("leaf", "node", None, None),
        P("leaf", "node", None, None),
        P("leaf", None),
        P("leaf", "node", None, None),
        P("leaf", "node", None, None),
        P("leaf", None, "node", None, None),
        P("leaf", "node", None, None),
        P("leaf", "node", None, None),
    )
    out_specs = P("leaf", "node", None, None)
    return jax.shard_map(shards, mesh=mesh, in_specs=in_specs, out_specs=out_specs, check_vma=False)
```
